128 devices in a mesh: grp: 8 (over z, core), row: 16 (over x, y).
Axes of the slice: x: 4, y: 4, z: 4, core: 2. Of those that a mesh axis runs over, the one named last changes fastest.
Arguments:
- embeddings: bfloat16 [131072, 256], P(('grp', 'row')), may hold values from -6 to 6
- neighbour_tile_mask: int32 [512, 8, 256, 256], P(('grp', 'row')), may hold values 0 or 1
- column_blocks: int32 [512, 8], P(('grp', 'row')), may hold values from 0 to 63, as said below
- seed_labels: int32 [131072], P(('grp', 'row')), may hold values from 0 to 64, as said below
Outputs:
- label_scores: float32 [64, 131072], P(None, ('grp', 'row'))
The draws below stay inside these ranges and needn't reach their ends.
Inputs may be any that keep to these rules, and one draw needn't show every extreme that they name: `column_blocks`: entry [r, k] names a block of r's group (r // 64) by its index in that group; block b of a group lies on the group's device b // 4 along row. The 8 column blocks of one row-block lie on 8 different devices and never include r itself, so a device receives at most 4 mirrored tiles from one device, at most one from each of its row-blocks; in every draw each device has a device that receives exactly 4 from it. `seed_labels`: 64 marks a node without a seed label.
All inputs are finite; a program needn't handle non-finite values. No bound on the sum of `neighbour_tile_mask` on one device may be relied on, other than what follows from the above.
Results may differ from the reference program's by a relative error of at most 0.00041.
Values may be sent and summed in bfloat16 or wider, within the bound.
No kernel may reach another device: no remote copies, remote signals or barrier semaphores. Data moves between devices by JAX's collectives and lax.ppermute only.
A program may use at most 128 MiB of HBM per device.

```python
import jax
import jax.numpy as jnp
from jax import lax

EMBEDDING_WIDTH = 256
CLASSES = 64
TILE_SIZE = 256
TILES_ROW = 8
STEPS = 2
BLOCKS_DEV = 4
GROUP_BLOCKS = 64
ROW_BLOCKS = 512
NODES = 131072
N_GRP = 8
N_ROW = 16


def draw_column_blocks(key, part):
    device_count = N_GRP * N_ROW
    key_favored, key_order, key_local, key_shift = jax.random.split(key, 4)
    favored = jax.random.randint(key_favored, (device_count, 1, 1), 0, N_ROW)
    peer_index = jnp.arange(N_ROW, dtype=jnp.int32)
    random_scores = jax.random.randint(key_order, (device_count, BLOCKS_DEV, N_ROW), 0, 1 << 20)
    ranking_scores = random_scores * N_ROW + peer_index
    ranking_scores = jnp.where(peer_index == favored, -1, ranking_scores)
    ranking = jnp.argsort(ranking_scores, axis=-1, stable=True).astype(jnp.int32)
    chosen = ranking[:, :, :TILES_ROW]
    local_block = jax.random.randint(key_local, (device_count, BLOCKS_DEV, TILES_ROW), 0, BLOCKS_DEV)
    shift_by = jax.random.randint(key_shift, (device_count, BLOCKS_DEV, TILES_ROW), 1, BLOCKS_DEV)
    self_member = (jnp.arange(device_count, dtype=jnp.int32) % N_ROW)[:, None, None]
    own_block = jnp.arange(BLOCKS_DEV, dtype=jnp.int32)[None, :, None]
    local_block = jnp.where(chosen == self_member, (own_block + shift_by) % BLOCKS_DEV, local_block)
    return (chosen * BLOCKS_DEV + local_block).reshape(ROW_BLOCKS, TILES_ROW).astype(jnp.int32)


def draw_seed_labels(key, part):
    key_chance, key_class = jax.random.split(key)
    position = jnp.arange(NODES, dtype=jnp.int32)
    chance = jax.random.randint(key_chance, (NODES,), 0, 1000)
    labeled = chance * NODES < 100 * NODES + 200 * position
    picked = jax.random.randint(key_class, (NODES,), 0, CLASSES)
    return jnp.where(labeled, picked, CLASSES).astype(jnp.int32)


def plant(array, stream_key, low, largest):
    longest = array.shape.index(max(array.shape))
    spots = []
    for shift in (0, 1):
        where = [jax.random.randint(jax.random.fold_in(stream_key, axis), (), 0, length) for axis, length in enumerate(array.shape)]
        where[longest] = (where[longest] + shift) % array.shape[longest]
        spots.append(tuple(where))
    return array.at[spots[0]].set(low).at[spots[1]].set(largest)


def level_of(rng, dims, cuts, low, top_value):
    level, own = 1.0, jax.random.fold_in(rng, 6)
    for dim, parts in cuts:
        steps = jnp.exp(jax.random.uniform(jax.random.fold_in(own, dim), (parts,), jnp.float32, low / len(cuts), top_value / len(cuts)))
        level = level * jnp.repeat(steps, dims[dim] // parts).reshape([-1 if axis == dim else 1 for axis in range(len(dims))])
    return level


def noise(key, shape, scale, bound, pieces=(), held_as=jnp.bfloat16):
    array = scale * jax.random.normal(key, shape, jnp.float32)
    if pieces:
        array = array * level_of(key, shape, pieces, -0.22, 0.18)
    return jnp.clip(array, -bound, bound).astype(held_as)


def setup_inputs(seed: int = 0) -> dict:
    keys = jax.random.split(jax.random.key(seed), 5)
    embeddings = noise(keys[0], (NODES, EMBEDDING_WIDTH), 1.0, 6.0, ((0, 128),))
    neighbour_tile_mask = plant((jax.random.randint(keys[1], (ROW_BLOCKS, TILES_ROW, TILE_SIZE, TILE_SIZE), 0, 4) < 3).astype(jnp.int32), jax.random.fold_in(keys[1], 1), 0, 1)
    column_blocks = draw_column_blocks(jax.random.fold_in(keys[4], 71), 0)
    seed_labels = draw_seed_labels(jax.random.fold_in(keys[4], 71), 0)
    return dict(embeddings=embeddings, neighbour_tile_mask=neighbour_tile_mask, column_blocks=column_blocks, seed_labels=seed_labels)


SOFTMAX_WARMTH = 0.1
PROPAGATION = 0.9

def reference(embeddings, neighbour_tile_mask, column_blocks, seed_labels):
    features = embeddings.astype(jnp.float32)
    unit_rows = (features * lax.rsqrt(lax.optimization_barrier(jnp.mean(features * features, axis=1, keepdims=True)) + 1e-06)).astype(jnp.bfloat16)
    unit_blocks = unit_rows.reshape(ROW_BLOCKS, TILE_SIZE, EMBEDDING_WIDTH)
    group_start = jnp.arange(ROW_BLOCKS, dtype=jnp.int32) // GROUP_BLOCKS * GROUP_BLOCKS
    global_cols = (group_start[:, None] + column_blocks).astype(jnp.int32)

    def tile_row(operand):
        own_block, columns, block_mask_tile = operand
        column_units = unit_blocks[columns]
        score_values = jnp.einsum('ie,kje->kij', own_block.astype(jnp.float32), column_units.astype(jnp.float32), precision=lax.Precision.HIGHEST)
        return jnp.where(block_mask_tile > 0, jnp.exp(score_values / (EMBEDDING_WIDTH * SOFTMAX_WARMTH)), jnp.zeros_like(score_values)).astype(jnp.bfloat16)
    affinity_matrix = lax.map(tile_row, (unit_blocks, global_cols, neighbour_tile_mask))
    row_sums = lax.optimization_barrier(jnp.sum(affinity_matrix, axis=(1, 3), dtype=jnp.float32))
    column_sums = lax.optimization_barrier(jnp.sum(affinity_matrix, axis=2, dtype=jnp.float32))
    mirror_degree = jax.ops.segment_sum(column_sums.reshape(ROW_BLOCKS * TILES_ROW, TILE_SIZE), global_cols.reshape(-1), num_segments=ROW_BLOCKS)
    degree = (1.0 + row_sums + mirror_degree).reshape(NODES)
    inverse_root = lax.rsqrt(degree)
    class_hits = (seed_labels[None, :] == jnp.arange(CLASSES, dtype=jnp.int32)[:, None]).astype(jnp.float32)
    counts = lax.optimization_barrier(jnp.sum(class_hits, axis=1))
    seed_field = class_hits * (NODES / (counts + 1.0))[:, None]
    label_field = seed_field
    for iteration in range(STEPS):
        spread = (label_field * inverse_root[None, :]).astype(jnp.bfloat16)
        spread_blocks = spread.reshape(CLASSES, ROW_BLOCKS, TILE_SIZE)

        def forward_row(operand):
            tiles_here, columns = operand
            column_spread = spread_blocks[:, columns]
            return jnp.einsum('kij,ckj->ci', tiles_here.astype(jnp.float32), column_spread.astype(jnp.float32), precision=lax.Precision.HIGHEST)

        def backward_row(operand):
            tiles_here, own_spread = operand
            product = jnp.einsum('kij,ci->kcj', tiles_here.astype(jnp.float32), own_spread.astype(jnp.float32), precision=lax.Precision.HIGHEST)
            return product.astype(jnp.bfloat16)
        forward = lax.map(forward_row, (affinity_matrix, global_cols))
        backward = lax.map(backward_row, (affinity_matrix, jnp.transpose(spread_blocks, (1, 0, 2)))).astype(jnp.float32)
        mirror = jax.ops.segment_sum(backward.reshape(ROW_BLOCKS * TILES_ROW, CLASSES, TILE_SIZE), global_cols.reshape(-1), num_segments=ROW_BLOCKS)
        summed = jnp.transpose(forward + mirror, (1, 0, 2)).reshape(CLASSES, NODES) + spread.astype(jnp.float32)
        label_field = PROPAGATION * inverse_root[None, :] * summed + (1.0 - PROPAGATION) * seed_field
    return label_field
```

```python
import functools

import jax
import jax.numpy as jnp
from jax import lax
from jax.experimental import pallas as pl
from jax.experimental.pallas import tpu as pltpu
from jax.sharding import PartitionSpec as P

CLASSES = 64
STEPS = 2
SOFTMAX_WARMTH = 0.1
PROPAGATION = 0.9
SIDE = 4
PEERS = SIDE * SIDE
BLOCKS = 4
TILES = 8
EDGE = 256
SLOTS = BLOCKS * CLASSES
EXTRA = 16


F32 = jnp.float32
BF16 = jnp.bfloat16
ANY = pl.BlockSpec(memory_space=pl.ANY)
SMEM = pl.BlockSpec(memory_space=pltpu.SMEM)
VMEM = pl.BlockSpec(memory_space=pltpu.VMEM)


def shift(value, dx, dy):
    pairs = [
        (a, ((a // SIDE + dx) % SIDE) * SIDE + (a % SIDE + dy) % SIDE) for a in range(PEERS)
    ]
    return lax.ppermute(value, "row", pairs)


def ring(value, dx, dy):
    half = value.shape[0] // 2
    before = shift(value, dx, dy)
    after = shift(value, -dx, -dy)
    far_low = shift(before[:half], dx, dy)
    far_high = shift(after[half:], -dx, -dy)
    return before, after, far_low, far_high


def gather_group(low, high):
    first_low = ring(low, 1, 0)
    first_high = ring(high, 0, 1)
    line_low = jnp.concatenate((low,) + first_low, axis=0)
    line_high = jnp.concatenate((high,) + first_high, axis=0)
    rest_low = ring(line_low, 0, 1)
    rest_high = ring(line_high, 1, 0)
    return (line_low,) + rest_low + (line_high,) + rest_high


def fetch(column, me, pieces, target, sem):
    device, block = column // BLOCKS, column % BLOCKS
    off_x = (device // SIDE - me // SIDE + SIDE) % SIDE
    off_y = (device % SIDE - me % SIDE + SIDE) % SIDE
    is_high = block >= 2
    first = jnp.where(is_high, off_y, off_x)
    second = jnp.where(is_high, off_x, off_y)
    place = jnp.where(first == 0, 0, jnp.where(first == 1, 2, jnp.where(first == 2, 3, 1)))
    slot = place * 2 + block % 2
    index = jnp.where(
        second == 0,
        0,
        jnp.where(second == 3, 1, jnp.where(second == 1, 2, jnp.where(slot < 4, 3, 4))),
    )
    slot = jnp.where(index == 4, slot - 4, slot)
    index = index + jnp.where(is_high, 5, 0)
    for number, piece in enumerate(pieces):

        @pl.when(index == number)
        def _():
            pltpu.make_async_copy(piece.at[slot], target, sem).start()


def unit_kernel(x_ref, full_ref, low_ref, high_ref):
    for block in range(BLOCKS):
        features = x_ref[pl.ds(block * EDGE, EDGE), :].astype(F32)
        mean = jnp.mean(features * features, axis=1, keepdims=True)
        unit = (features * lax.rsqrt(mean + 1e-06)).astype(BF16)
        full_ref[block] = unit
        (low_ref if block < 2 else high_ref)[block % 2] = unit


def tile_kernel(cols, me_ref, mask_ref, unit_ref, *rest):
    pieces = rest[:10]
    tiles_ref, rows_ref, sums_ref, held, total, sems = rest[10:]
    block = pl.program_id(0)
    me = me_ref[0]

    @pl.when(block == 0)
    def _():
        @pl.loop(0, BLOCKS * TILES)
        def _(t):
            fetch(cols[t], me, pieces, held.at[t], sems.at[t])

        sums_ref[...] = jnp.zeros_like(sums_ref)

    own = unit_ref[0]
    scale = 1.0 / (own.shape[1] * SOFTMAX_WARMTH)
    lane_block = lax.broadcasted_iota(jnp.int32, (BLOCKS, EDGE), 0)
    for k in range(TILES):
        t = block * TILES + k
        pltpu.make_async_copy(pieces[0].at[0], held.at[t], sems.at[t]).wait()
        score = lax.dot_general(
            own, held[t], (((1,), (1,)), ((), ())), preferred_element_type=F32
        )
        tile = jnp.where(mask_ref[0, k] > 0, jnp.exp(score * scale), 0.0).astype(BF16)
        tiles_ref[0, k] = tile
        wide = tile.astype(F32)
        column = cols[t]
        sums = jnp.sum(wide, axis=0, keepdims=True)
        sums_ref[column // BLOCKS] += jnp.where(lane_block == column % BLOCKS, sums, 0.0)
        if k == 0:
            total[...] = wide
        else:
            total[...] += wide
    folded = total[:, : EDGE // 2] + total[:, EDGE // 2 :]
    rows_ref[0] = jnp.sum(folded.T, axis=0, keepdims=True)


def seed_block(labels_row, weight):
    classes = lax.broadcasted_iota(jnp.int32, (CLASSES, EDGE), 0)
    return jnp.where(classes == labels_row, weight, 0.0)


def first_send_kernel(
    cols, tiles_ref, rows_ref, sums_ref, labels_ref, weight_ref, send_ref, root_ref, spread_ref
):
    block = pl.program_id(0)

    @pl.when(block == 0)
    def _():
        degree = 1.0 + jnp.sum(sums_ref[...], axis=0)
        for b in range(BLOCKS):
            root = lax.rsqrt(degree[b : b + 1] + rows_ref[b])
            root_ref[b] = root
            seed = seed_block(labels_ref[b : b + 1, :], weight_ref[...])
            spread_ref[b] = (seed * root).astype(BF16)
        values = [
            jnp.sum(spread_ref[b].astype(F32), axis=0, keepdims=True) for b in range(BLOCKS)
        ]
        values = jnp.concatenate(values + [jnp.zeros((EXTRA - BLOCKS, EDGE), F32)], axis=0)
        values = values.astype(BF16)
        for p in range(PEERS):
            send_ref[p, SLOTS:, :] = values

    mirror_terms(cols, block, spread_ref[block], tiles_ref, send_ref)


def mirror_terms(cols, block, spread, tiles_ref, send_ref):
    for k in range(TILES):
        term = jnp.dot(spread, tiles_ref[0, k], preferred_element_type=F32)
        device = cols[block * TILES + k] // BLOCKS
        start = pl.multiple_of(block * CLASSES, CLASSES)
        send_ref[device, pl.ds(start, CLASSES), :] = term.astype(BF16)


def second_send_kernel(cols, tiles_ref, spread_ref, send_ref):
    mirror_terms(cols, pl.program_id(0), spread_ref[0], tiles_ref, send_ref)


def add_mirrored(targets, block, terms_ref, mirror):
    @pl.when(block == 0)
    def _():
        mirror[...] = jnp.zeros_like(mirror)

    for p in range(BLOCKS):
        for j in range(BLOCKS):
            target = targets[(block * BLOCKS + p) * BLOCKS + j]

            @pl.when(target >= 0)
            def _():
                mirror[target] += terms_ref[p, j * CLASSES : (j + 1) * CLASSES, :].astype(F32)


def forward_term(spread, tile):
    return lax.dot_general(spread, tile, (((1,), (1,)), ((), ())), preferred_element_type=F32)


def updated(block, spread_ref, forward, mirror, root_ref, labels_ref, weight_ref):
    summed = forward[block] + mirror[block] + spread_ref[block].astype(F32)
    root = root_ref[block]
    seed = seed_block(labels_ref[block : block + 1, :], weight_ref[...])
    return PROPAGATION * root * summed + (1.0 - PROPAGATION) * seed, root


def first_update_kernel(
    cols,
    targets,
    tiles_ref,
    terms_ref,
    values_ref,
    group_labels_ref,
    spread_ref,
    root_ref,
    labels_ref,
    weight_ref,
    full_ref,
    low_ref,
    high_ref,
    forward,
    mirror,
    values,
):
    block = pl.program_id(0)

    @pl.when(block == 0)
    def _():
        values[...] = values_ref[...].astype(F32)

    add_mirrored(targets, block, terms_ref, mirror)
    for k in range(TILES):
        column = cols[block * TILES + k]
        device, row = column // BLOCKS, column % BLOCKS
        source = seed_block(
            group_labels_ref[device, pl.ds(row, 1), :], values[device, pl.ds(row, 1), :]
        )
        term = forward_term(source.astype(BF16), tiles_ref[0, k])
        if k == 0:
            forward[block] = term
        else:
            forward[block] += term

    @pl.when(block == BLOCKS - 1)
    def _():
        for b in range(BLOCKS):
            field, root = updated(b, spread_ref, forward, mirror, root_ref, labels_ref, weight_ref)
            spread = (field * root).astype(BF16)
            full_ref[b] = spread
            (low_ref if b < 2 else high_ref)[b % 2] = spread


def last_update_kernel(
    cols, targets, me_ref, tiles_ref, terms_ref, spread_ref, root_ref, labels_ref, weight_ref, *rest
):
    pieces = rest[:10]
    out_ref, forward, mirror, held, sems = rest[10:]
    block = pl.program_id(0)

    @pl.when(block == 0)
    def _():
        @pl.loop(0, BLOCKS * TILES)
        def _(t):
            fetch(cols[t], me_ref[0], pieces, held.at[t], sems.at[t])

    add_mirrored(targets, block, terms_ref, mirror)
    for k in range(TILES):
        t = block * TILES + k
        pltpu.make_async_copy(pieces[0].at[0], held.at[t], sems.at[t]).wait()
        term = forward_term(held[t], tiles_ref[0, k])
        if k == 0:
            forward[block] = term
        else:
            forward[block] += term

    @pl.when(block == BLOCKS - 1)
    def _():
        for b in range(BLOCKS):
            field, _ = updated(b, spread_ref, forward, mirror, root_ref, labels_ref, weight_ref)
            out_ref[:, b * EDGE : (b + 1) * EDGE] = field


def whole(shape):
    return pl.BlockSpec(shape, lambda i: (0,) * len(shape))


def step(*shape):
    return pl.BlockSpec((1,) + shape, lambda i: (i,) + (0,) * len(shape))


def call(kernel, name, grid, in_specs, out_specs, out_shape, scratch=(), flops=0, moved=0):
    return pl.pallas_call(
        kernel,
        name=name,
        grid=grid,
        in_specs=in_specs,
        out_specs=out_specs,
        out_shape=[jax.ShapeDtypeStruct(s, d) for s, d in out_shape],
        scratch_shapes=list(scratch),
        cost_estimate=pl.CostEstimate(flops=flops, bytes_accessed=moved, transcendentals=0),
        compiler_params=pltpu.CompilerParams(vmem_limit_bytes=40 << 20),
    )


def exchange(value, axis="row"):
    return lax.all_to_all(value, axis, split_axis=0, concat_axis=0, tiled=True)


def local(embeddings, neighbour_tile_mask, column_blocks, seed_labels):
    width = embeddings.shape[1]
    groups = lax.axis_size("grp")
    node_total = BLOCKS * EDGE * PEERS * groups
    me = lax.axis_index("row").astype(jnp.int32)
    cols = column_blocks.reshape(BLOCKS * TILES)
    labels = seed_labels.reshape(BLOCKS, EDGE)

    unit, unit_low, unit_high = call(
        unit_kernel,
        "unit",
        (),
        [VMEM],
        [VMEM] * 3,
        [((BLOCKS, EDGE, width), BF16), ((2, EDGE, width), BF16), ((2, EDGE, width), BF16)],
        moved=3 << 19,
    )(embeddings)
    pieces = gather_group(unit_low, unit_high)

    packed = jnp.concatenate((seed_labels, jnp.pad(cols, (0, 992)))).reshape(1, 16, 128)
    packed = exchange(jnp.broadcast_to(packed, (PEERS, 16, 128)))
    group_labels = packed[:, :8].reshape(PEERS, BLOCKS, EDGE)
    group_cols = packed[:, 8, : BLOCKS * TILES].reshape(PEERS, BLOCKS, TILES)
    targets = jnp.sum(
        jnp.where(group_cols // BLOCKS == me, group_cols % BLOCKS + 1, 0), axis=2
    ).reshape(-1) - 1
    classes = jnp.arange(128, dtype=jnp.int32)
    counts = jnp.sum(
        (group_labels.reshape(-1)[None, :] == classes[:, None]).astype(jnp.int32), axis=1
    )
    counts = exchange(jnp.broadcast_to(counts.reshape(1, 1, 128), (groups, 1, 128)), "grp")
    counts = jnp.sum(counts, axis=(0, 1))[:CLASSES].astype(F32)
    weight = (node_total / (counts + 1.0)).reshape(CLASSES, 1)

    tiles_shape = (BLOCKS, TILES, EDGE, EDGE)
    tiles, rows, sums = call(
        tile_kernel,
        "tiles",
        (BLOCKS,),
        [SMEM, SMEM, step(TILES, EDGE, EDGE), step(EDGE, width)] + [ANY] * 10,
        [step(TILES, EDGE, EDGE), step(1, EDGE), whole((PEERS, BLOCKS, EDGE))],
        [(tiles_shape, BF16), ((BLOCKS, 1, EDGE), F32), ((PEERS, BLOCKS, EDGE), F32)],
        [
            pltpu.VMEM((BLOCKS * TILES, EDGE, width), BF16),
            pltpu.VMEM((EDGE, EDGE), F32),
            pltpu.SemaphoreType.DMA((BLOCKS * TILES,)),
        ],
        flops=2 << 30,
        moved=16 << 20,
    )(cols, me.reshape(1), neighbour_tile_mask, unit, *pieces)
    sums = exchange(sums)

    send_rows = SLOTS + EXTRA
    send, root, spread = call(
        first_send_kernel,
        "first_send",
        (BLOCKS,),
        [
            SMEM,
            step(TILES, EDGE, EDGE),
            whole((BLOCKS, 1, EDGE)),
            whole((PEERS, BLOCKS, EDGE)),
            whole((BLOCKS, EDGE)),
            whole((CLASSES, 1)),
        ],
        [
            whole((PEERS, send_rows, EDGE)),
            whole((BLOCKS, 1, EDGE)),
            whole((BLOCKS, CLASSES, EDGE)),
        ],
        [
            ((PEERS, send_rows, EDGE), BF16),
            ((BLOCKS, 1, EDGE), F32),
            ((BLOCKS, CLASSES, EDGE), BF16),
        ],
        flops=1 << 28,
        moved=6 << 20,
    )(cols, tiles, rows, sums, labels, weight)
    arrived = exchange(send)

    field_shape = (BLOCKS, CLASSES, EDGE)
    half_shape = (2, CLASSES, EDGE)
    spread, spread_low, spread_high = call(
        first_update_kernel,
        "first_update",
        (BLOCKS,),
        [
            SMEM,
            SMEM,
            step(TILES, EDGE, EDGE),
            pl.BlockSpec((BLOCKS, send_rows, EDGE), lambda i: (i, 0, 0)),
            pl.BlockSpec((PEERS, EXTRA, EDGE), lambda i: (0, SLOTS // EXTRA, 0)),
            whole((PEERS, BLOCKS, EDGE)),
            whole(field_shape),
            whole((BLOCKS, 1, EDGE)),
            whole((BLOCKS, EDGE)),
            whole((CLASSES, 1)),
        ],
        [whole(field_shape), whole(half_shape), whole(half_shape)],
        [(field_shape, BF16), (half_shape, BF16), (half_shape, BF16)],
        [
            pltpu.VMEM(field_shape, F32),
            pltpu.VMEM(field_shape, F32),
            pltpu.VMEM((PEERS, EXTRA, EDGE), F32),
        ],
        flops=1 << 28,
        moved=7 << 20,
    )(cols, targets, tiles, arrived, arrived, group_labels, spread, root, labels, weight)
    pieces = gather_group(spread_low, spread_high)

    (send,) = call(
        second_send_kernel,
        "second_send",
        (BLOCKS,),
        [SMEM, step(TILES, EDGE, EDGE), step(CLASSES, EDGE)],
        [whole((PEERS, SLOTS, EDGE))],
        [((PEERS, SLOTS, EDGE), BF16)],
        flops=1 << 28,
        moved=6 << 20,
    )(cols, tiles, spread)
    arrived = exchange(send)

    (out,) = call(
        last_update_kernel,
        "last_update",
        (BLOCKS,),
        [
            SMEM,
            SMEM,
            SMEM,
            step(TILES, EDGE, EDGE),
            pl.BlockSpec((BLOCKS, SLOTS, EDGE), lambda i: (i, 0, 0)),
            whole(field_shape),
            whole((BLOCKS, 1, EDGE)),
            whole((BLOCKS, EDGE)),
            whole((CLASSES, 1)),
        ]
        + [ANY] * 10,
        [whole((CLASSES, BLOCKS * EDGE))],
        [((CLASSES, BLOCKS * EDGE), F32)],
        [
            pltpu.VMEM(field_shape, F32),
            pltpu.VMEM(field_shape, F32),
            pltpu.VMEM((BLOCKS * TILES, CLASSES, EDGE), BF16),
            pltpu.SemaphoreType.DMA((BLOCKS * TILES,)),
        ],
        flops=1 << 28,
        moved=10 << 20,
    )(cols, targets, me.reshape(1), tiles, arrived, spread, root, labels, weight, *pieces)
    return out


def solution(mesh):
    return jax.shard_map(
        local,
        mesh=mesh,
        in_specs=(
            P(("grp", "row"), None),
            P(("grp", "row"), None, None, None),
            P(("grp", "row"), None),
            P(("grp", "row")),
        ),
        out_specs=P(None, ("grp", "row")),
        check_vma=False,
    )
```

```python
import functools

import jax
import jax.numpy as jnp
from jax import lax
from jax.experimental import pallas as pl
from jax.experimental.pallas import tpu as pltpu
from jax.sharding import PartitionSpec as P

CLASSES = 64
STEPS = 2
SOFTMAX_WARMTH = 0.1
LOG2E = 1.4426950408889634
PROPAGATION = 0.9
SIDE = 4
PEERS = SIDE * SIDE
BLOCKS = 4
TILES = 8
EDGE = 256
SLOTS = BLOCKS * CLASSES
EXTRA = 16
GRANT = 62 << 20
PIECES = 16


F32 = jnp.float32
BF16 = jnp.bfloat16
ANY = pl.BlockSpec(memory_space=pl.ANY)
HBM = pl.BlockSpec(memory_space=pltpu.HBM)
SMEM = pl.BlockSpec(memory_space=pltpu.SMEM)
VMEM = pl.BlockSpec(memory_space=pltpu.VMEM)


def shift(value, dx, dy):
    pairs = [
        (a, ((a // SIDE + dx) % SIDE) * SIDE + (a % SIDE + dy) % SIDE) for a in range(PEERS)
    ]
    return lax.ppermute(value, "row", pairs)


def line_of(buffer, value, dx, dy, relay):
    before = shift(value, dx, dy)
    after = shift(value, -dx, -dy)
    if relay:
        far = [shift(before[:1], dx, dy), shift(after[1:], -dx, -dy)]
    else:
        far = [shift(value, 2 * dx, 2 * dy)]
    near = lax.dynamic_update_slice(buffer, before, (2,) + (0,) * (value.ndim - 1))
    return near, jnp.concatenate([after] + far, axis=0)


def spread_line(near, far, dx, dy, hold):
    near_before, near_after = shift(near, dx, dy), shift(near, -dx, -dy)
    far_before, far_after = shift(far, dx, dy), shift(far, -dx, -dy)
    near_before, far_after = hold(near_before, far_after)
    return (
        near,
        far,
        near_before,
        far_before,
        near_after,
        far_after,
        shift(near_before, dx, dy),
        shift(far_after, -dx, -dy),
    )


def gather_group(low, high, low_buffer, high_buffer, relay, hold=lambda *held: held):
    low_line = line_of(low_buffer, low, 1, 0, relay)
    high_line = line_of(high_buffer, high, 0, 1, relay)
    return spread_line(*low_line, 0, 1, hold) + spread_line(*high_line, 1, 0, hold)


def places(cols, me):
    device, block = cols // BLOCKS, cols % BLOCKS
    off_x = (device // SIDE - me // SIDE + SIDE) % SIDE
    off_y = (device % SIDE - me % SIDE + SIDE) % SIDE
    is_high = block >= 2
    first = jnp.where(is_high, off_y, off_x)
    second = jnp.where(is_high, off_x, off_y)
    part = jnp.where(first == 0, 0, jnp.where(first == 1, 2, jnp.where(first == 2, 3, 1)))
    line = jnp.where(second == 0, 0, jnp.where(second == 1, 2, jnp.where(second == 2, 3, 1)))
    number = line * 2 + part // 2 + jnp.where(is_high, 8, 0)
    return number * SIDE + (part % 2) * 2 + block % 2


def fetch(place, pieces, target, sem):
    number, slot = place // SIDE, place % SIDE

    def pick(low, high):
        if high - low == 1:
            pltpu.make_async_copy(pieces[low].at[slot], target, sem).start()
            return
        middle = (low + high) // 2
        lax.cond(number < middle, lambda: pick(low, middle), lambda: pick(middle, high))

    pick(0, PIECES)


def fetch_row(table, block, pieces, held, sems):
    for k in range(TILES):
        slot = block % 2 * TILES + k
        fetch(table[block * TILES + k], pieces, held.at[slot], sems.at[slot])


def turn_row(table, block, pieces, held, sems):
    @pl.when(block == 0)
    def _():
        fetch_row(table, block, pieces, held, sems)

    @pl.when(block < BLOCKS - 1)
    def _():
        fetch_row(table, block + 1, pieces, held, sems)

    for k in range(TILES):
        slot = block % 2 * TILES + k
        pltpu.make_async_copy(pieces[0].at[0], held.at[slot], sems.at[slot]).wait()


def load_tiles(block, tiles_ref, tiles, sems):
    @pl.when(block == 0)
    def _():
        for b in range(BLOCKS):
            pltpu.make_async_copy(tiles_ref.at[b], tiles.at[b], sems.at[b]).start()

    pltpu.make_async_copy(tiles_ref.at[block], tiles.at[block], sems.at[block]).wait()


def unit_kernel(x_ref, full_ref, low_ref, high_ref, low_line_ref, high_line_ref):
    for block in range(BLOCKS):
        features = x_ref[pl.ds(block * EDGE, EDGE), :].astype(F32)
        mean = jnp.mean(features * features, axis=1, keepdims=True)
        unit = (features * lax.rsqrt(mean + 1e-06)).astype(BF16)
        full_ref[block] = unit
        (low_ref if block < 2 else high_ref)[block % 2] = unit
        (low_line_ref if block < 2 else high_line_ref)[block % 2] = unit


def tile_kernel(cols, table, mask_ref, unit_ref, *rest):
    pieces = rest[:PIECES]
    tiles_ref, rows_ref, sums_ref, held, sems = rest[PIECES:]
    block = pl.program_id(0)
    turn_row(table, block, pieces, held, sems)

    @pl.when(block == 0)
    def _():
        sums_ref[...] = jnp.zeros_like(sums_ref)

    own = unit_ref[0]
    scale = LOG2E / (own.shape[1] * SOFTMAX_WARMTH)
    lane_block = lax.broadcasted_iota(jnp.int32, (BLOCKS, EDGE), 0)
    ones = jnp.ones((8, EDGE), BF16)
    rows = jnp.zeros((8, EDGE), F32)
    for k in range(TILES):
        score = lax.dot_general(
            own, held[block % 2 * TILES + k], (((1,), (1,)), ((), ())), preferred_element_type=F32
        )
        tile = jnp.where(mask_ref[0, k] > 0, jnp.exp2(score * scale), 0.0).astype(BF16)
        tiles_ref[0, k] = tile
        number = cols[block * TILES + k]
        sums = jnp.dot(ones, tile, preferred_element_type=F32)[:1]
        sums_ref[number // BLOCKS] += jnp.where(lane_block == number % BLOCKS, sums, 0.0)
        rows += lax.dot_general(
            ones, tile, (((1,), (1,)), ((), ())), preferred_element_type=F32
        )
    rows_ref[0] = rows[:1]


def seed_block(labels_row, weight):
    classes = lax.broadcasted_iota(jnp.int32, (CLASSES, EDGE), 0).astype(labels_row.dtype)
    return jnp.where(classes == labels_row, weight, 0.0)


def first_send_kernel(
    cols,
    tiles_ref,
    rows_ref,
    sums_ref,
    labels_ref,
    weight_ref,
    send_ref,
    root_ref,
    spread_ref,
    tiles,
    sems,
):
    block = pl.program_id(0)
    load_tiles(block, tiles_ref, tiles, sems)

    @pl.when(block == 0)
    def _():
        degree = 1.0 + jnp.sum(sums_ref[...], axis=0)
        for b in range(BLOCKS):
            root = lax.rsqrt(degree[b : b + 1] + rows_ref[b])
            root_ref[b] = root
            seed = seed_block(labels_ref[b : b + 1, :], weight_ref[...])
            spread_ref[b] = (seed * root).astype(BF16)
        values = [
            jnp.sum(spread_ref[b].astype(F32), axis=0, keepdims=True) for b in range(BLOCKS)
        ]
        values += [labels_ref[...].astype(F32)]
        values = jnp.concatenate(values + [jnp.zeros((EXTRA - 2 * BLOCKS, EDGE), F32)], axis=0)
        values = values.astype(BF16)
        for p in range(PEERS):
            send_ref[p, SLOTS:, :] = values

    mirror_terms(cols, block, spread_ref[block], tiles, send_ref)


def mirror_terms(cols, block, spread, tiles, send_ref):
    for k in range(TILES):
        term = jnp.dot(spread, tiles[block, k], preferred_element_type=F32)
        device = cols[block * TILES + k] // BLOCKS
        start = pl.multiple_of(block * CLASSES, CLASSES)
        send_ref[device, pl.ds(start, CLASSES), :] = term.astype(BF16)


def second_send_kernel(cols, tiles_ref, spread_ref, send_ref, tiles, sems):
    block = pl.program_id(0)
    load_tiles(block, tiles_ref, tiles, sems)
    mirror_terms(cols, block, spread_ref[0], tiles, send_ref)


def add_mirrored(targets, block, terms_ref, mirror):
    @pl.when(block == 0)
    def _():
        mirror[...] = jnp.zeros_like(mirror)

    for p in range(BLOCKS):
        for j in range(BLOCKS):
            target = targets[(block * BLOCKS + p) * BLOCKS + j]

            @pl.when(target >= 0)
            def _():
                mirror[target] += terms_ref[p, j * CLASSES : (j + 1) * CLASSES, :].astype(F32)


def forward_term(spread, tile):
    return lax.dot_general(spread, tile, (((1,), (1,)), ((), ())), preferred_element_type=F32)


def updated(block, spread_ref, forward, mirror, root_ref, labels_ref, weight_ref):
    summed = forward[block] + mirror[block] + spread_ref[block].astype(F32)
    root = root_ref[block]
    seed = seed_block(labels_ref[block : block + 1, :], weight_ref[...])
    return PROPAGATION * root * summed + (1.0 - PROPAGATION) * seed, root


def first_update_kernel(
    cols,
    targets,
    tiles_ref,
    terms_ref,
    values_ref,
    spread_ref,
    root_ref,
    labels_ref,
    weight_ref,
    full_ref,
    low_ref,
    high_ref,
    low_line_ref,
    high_line_ref,
    forward,
    mirror,
    values,
    tiles,
    sems,
):
    block = pl.program_id(0)
    load_tiles(block, tiles_ref, tiles, sems)

    @pl.when(block == 0)
    def _():
        values[...] = values_ref[...].astype(F32)

    add_mirrored(targets, block, terms_ref, mirror)
    for k in range(TILES):
        column = cols[block * TILES + k]
        device, row = column // BLOCKS, column % BLOCKS
        source = seed_block(
            values[device, pl.ds(row + BLOCKS, 1), :], values[device, pl.ds(row, 1), :]
        )
        term = forward_term(source.astype(BF16), tiles[block, k])
        if k == 0:
            forward[block] = term
        else:
            forward[block] += term

    @pl.when(block == BLOCKS - 1)
    def _():
        for b in range(BLOCKS):
            field, root = updated(b, spread_ref, forward, mirror, root_ref, labels_ref, weight_ref)
            spread = (field * root).astype(BF16)
            full_ref[b] = spread
            (low_ref if b < 2 else high_ref)[b % 2] = spread
            (low_line_ref if b < 2 else high_line_ref)[b % 2] = spread


def last_update_kernel(
    table, targets, tiles_ref, terms_ref, spread_ref, root_ref, labels_ref, weight_ref, *rest
):
    pieces = rest[:PIECES]
    out_ref, forward, mirror, held, sems, tiles, tile_sems = rest[PIECES:]
    block = pl.program_id(0)
    load_tiles(block, tiles_ref, tiles, tile_sems)
    turn_row(table, block, pieces, held, sems)
    add_mirrored(targets, block, terms_ref, mirror)
    for k in range(TILES):
        term = forward_term(held[block % 2 * TILES + k], tiles[block, k])
        if k == 0:
            forward[block] = term
        else:
            forward[block] += term

    @pl.when(block == BLOCKS - 1)
    def _():
        for b in range(BLOCKS):
            field, _ = updated(b, spread_ref, forward, mirror, root_ref, labels_ref, weight_ref)
            out_ref[:, b * EDGE : (b + 1) * EDGE] = field


def whole(shape):
    return pl.BlockSpec(shape, lambda i: (0,) * len(shape))


def step(*shape):
    return pl.BlockSpec((1,) + shape, lambda i: (i,) + (0,) * len(shape))


def call(
    kernel, name, grid, in_specs, out_specs, out_shape, scratch=(), flops=0, moved=0, grant=GRANT
):
    return pl.pallas_call(
        kernel,
        name=name,
        grid=grid,
        in_specs=in_specs,
        out_specs=out_specs,
        out_shape=[jax.ShapeDtypeStruct(s, d) for s, d in out_shape],
        scratch_shapes=list(scratch),
        cost_estimate=pl.CostEstimate(flops=flops, bytes_accessed=moved, transcendentals=0),
        compiler_params=pltpu.CompilerParams(vmem_limit_bytes=grant),
    )


def exchange(value, axis="row"):
    return lax.all_to_all(value, axis, split_axis=0, concat_axis=0, tiled=True)


def local(embeddings, neighbour_tile_mask, column_blocks, seed_labels):
    width = embeddings.shape[1]
    groups = lax.axis_size("grp")
    node_total = BLOCKS * EDGE * PEERS * groups
    me = lax.axis_index("row").astype(jnp.int32)
    cols = column_blocks.reshape(BLOCKS * TILES)
    labels = seed_labels.reshape(BLOCKS, EDGE)

    table = places(cols, me)

    half_shape, line_shape = (2, EDGE, width), (SIDE, EDGE, width)
    unit, *parts = call(
        unit_kernel,
        "unit",
        (),
        [VMEM],
        [VMEM] * 5,
        [
            ((BLOCKS, EDGE, width), BF16),
            (half_shape, BF16),
            (half_shape, BF16),
            (line_shape, BF16),
            (line_shape, BF16),
        ],
        moved=3 << 19,
    )(embeddings)
    classes = jnp.arange(CLASSES, dtype=jnp.int32)
    hits = jnp.sum((labels[None] == classes[:, None, None]).astype(jnp.int32), axis=(1, 2))
    packed = jnp.concatenate((hits, jnp.pad(cols, (0, 128 - CLASSES - BLOCKS * TILES))))
    packed = exchange(
        jnp.broadcast_to(packed.reshape(1, 1, 128), (groups * PEERS, 1, 128)), ("grp", "row")
    ).reshape(groups * PEERS, 128)
    pieces = gather_group(
        *parts, relay=True, hold=lambda *held: lax.optimization_barrier(held + (packed,))[:-1]
    )
    counts = jnp.sum(packed[:, :CLASSES], axis=0).astype(F32)
    weight = (node_total / (counts + 1.0)).reshape(CLASSES, 1)
    group_cols = lax.dynamic_slice(
        packed, (lax.axis_index("grp") * PEERS, CLASSES), (PEERS, BLOCKS * TILES)
    ).reshape(PEERS, BLOCKS, TILES)
    targets = jnp.sum(
        jnp.where(group_cols // BLOCKS == me, group_cols % BLOCKS + 1, 0), axis=2
    ).reshape(-1) - 1

    tiles_shape = (BLOCKS, TILES, EDGE, EDGE)
    tiles, rows, sums = call(
        tile_kernel,
        "tiles",
        (BLOCKS,),
        [SMEM, SMEM, step(TILES, EDGE, EDGE), step(EDGE, width)] + [ANY] * PIECES,
        [step(TILES, EDGE, EDGE), step(1, EDGE), whole((PEERS, BLOCKS, EDGE))],
        [(tiles_shape, BF16), ((BLOCKS, 1, EDGE), F32), ((PEERS, BLOCKS, EDGE), F32)],
        [
            pltpu.VMEM((2 * TILES, EDGE, width), BF16),
            pltpu.SemaphoreType.DMA((2 * TILES,)),
        ],
        flops=2 << 30,
        moved=16 << 20,
    )(cols, table, neighbour_tile_mask, unit, *pieces)
    tiles_scratch = [pltpu.VMEM(tiles_shape, BF16), pltpu.SemaphoreType.DMA((BLOCKS,))]
    sums = exchange(sums)

    send_rows = SLOTS + EXTRA
    send, root, spread = call(
        first_send_kernel,
        "first_send",
        (BLOCKS,),
        [
            SMEM,
            HBM,
            whole((BLOCKS, 1, EDGE)),
            whole((PEERS, BLOCKS, EDGE)),
            whole((BLOCKS, EDGE)),
            whole((CLASSES, 1)),
        ],
        [
            whole((PEERS, send_rows, EDGE)),
            whole((BLOCKS, 1, EDGE)),
            whole((BLOCKS, CLASSES, EDGE)),
        ],
        [
            ((PEERS, send_rows, EDGE), BF16),
            ((BLOCKS, 1, EDGE), F32),
            ((BLOCKS, CLASSES, EDGE), BF16),
        ],
        tiles_scratch,
        flops=1 << 28,
        moved=6 << 20,
    )(cols, tiles, rows, sums, labels, weight)
    arrived = exchange(send)

    field_shape = (BLOCKS, CLASSES, EDGE)
    half_shape = (2, CLASSES, EDGE)
    spread, *parts = call(
        first_update_kernel,
        "first_update",
        (BLOCKS,),
        [
            SMEM,
            SMEM,
            HBM,
            pl.BlockSpec((BLOCKS, send_rows, EDGE), lambda i: (i, 0, 0)),
            pl.BlockSpec((PEERS, EXTRA, EDGE), lambda i: (0, SLOTS // EXTRA, 0)),
            whole(field_shape),
            whole((BLOCKS, 1, EDGE)),
            whole((BLOCKS, EDGE)),
            whole((CLASSES, 1)),
        ],
        [whole(field_shape)] + [whole(half_shape)] * 2 + [whole(field_shape)] * 2,
        [(field_shape, BF16)] + [(half_shape, BF16)] * 2 + [(field_shape, BF16)] * 2,
        [
            pltpu.VMEM(field_shape, F32),
            pltpu.VMEM(field_shape, F32),
            pltpu.VMEM((PEERS, EXTRA, EDGE), F32),
        ]
        + tiles_scratch,
        flops=1 << 28,
        moved=7 << 20,
    )(cols, targets, tiles, arrived, arrived, spread, root, labels, weight)
    pieces = gather_group(*parts, relay=False)

    (send,) = call(
        second_send_kernel,
        "second_send",
        (BLOCKS,),
        [SMEM, HBM, step(CLASSES, EDGE)],
        [whole((PEERS, SLOTS, EDGE))],
        [((PEERS, SLOTS, EDGE), BF16)],
        tiles_scratch,
        flops=1 << 28,
        moved=6 << 20,
    )(cols, tiles, spread)
    arrived = exchange(send)

    (out,) = call(
        last_update_kernel,
        "last_update",
        (BLOCKS,),
        [
            SMEM,
            SMEM,
            HBM,
            pl.BlockSpec((BLOCKS, SLOTS, EDGE), lambda i: (i, 0, 0)),
            whole(field_shape),
            whole((BLOCKS, 1, EDGE)),
            whole((BLOCKS, EDGE)),
            whole((CLASSES, 1)),
        ]
        + [ANY] * PIECES,
        [whole((CLASSES, BLOCKS * EDGE))],
        [((CLASSES, BLOCKS * EDGE), F32)],
        [
            pltpu.VMEM(field_shape, F32),
            pltpu.VMEM(field_shape, F32),
            pltpu.VMEM((2 * TILES, CLASSES, EDGE), BF16),
            pltpu.SemaphoreType.DMA((2 * TILES,)),
        ]
        + tiles_scratch,
        flops=1 << 28,
        moved=10 << 20,
    )(table, targets, tiles, arrived, spread, root, labels, weight, *pieces)
    return out


def solution(mesh):
    return jax.shard_map(
        local,
        mesh=mesh,
        in_specs=(
            P(("grp", "row"), None),
            P(("grp", "row"), None, None, None),
            P(("grp", "row"), None),
            P(("grp", "row")),
        ),
        out_specs=P(None, ("grp", "row")),
        check_vma=False,
    )
```
